256 devices in a mesh: track: 64 (over y, z, core), det: 4 (over x).
Axes of the slice: x: 4, y: 4, z: 8, core: 2. Of those that a mesh axis runs over, the one named last changes fastest.
Arguments:
- jac: float32 [32768, 12, 512], P('track', None, 'det'), may hold values from -1.75 to 1.75
- obs: float32 [32768, 512], P('track', 'det'), may hold values from -6 to 6
- match: int32 [32768], P('track'), may hold values from 0 to 32767, as said below
- tile_knot: int32 [32768], P('track'), may hold values from 0 to 127
- tile_frac: float32 [32768], P('track'), may hold values from 0 to 1
Outputs:
- knot_field: float32 [12, 8192], P(None, 'track')
- tie_residual: float32 [32768, 512], P('track', 'det')
The draws below stay inside these ranges and needn't reach their ends.
Inputs may be any that keep to these rules, and one draw needn't show every extreme that they name: match[match[i]] = i and match[i] != i; the tiles of each index of track cross exactly 8 tiles of every index of track, itself included.
All inputs are finite; a program needn't handle non-finite values.
Results may differ from the reference program's by a relative error of at most 0.0001.
Values sent between devices are 32-bit elements; how exact they have to be, the bound alone decides.
A program may use at most 64 MiB of HBM per device.

```python
import jax
import jax.numpy as jnp
from jax import lax

W = 512
P_SIZE = 12
TILE_DEV = 512
KNOT_DEV = 128
ITERS = 4
TILES = 32768
KNOTS = 8192
PEER = 8
N_TRACK = 64


def draw_match(key, part):
    subkeys = jax.random.split(key, N_TRACK)
    shuffled = jax.vmap(lambda single: jax.random.permutation(single, TILE_DEV))(subkeys).astype(jnp.int32)
    slot_pos = jnp.arange(TILE_DEV, dtype=jnp.int32)
    device_col = jnp.arange(N_TRACK, dtype=jnp.int32)[:, None]
    peer_index = jnp.broadcast_to((slot_pos // PEER)[None, :], (N_TRACK, TILE_DEV))
    within = jnp.broadcast_to((slot_pos % PEER)[None, :], (N_TRACK, TILE_DEV))
    paired = jnp.where(peer_index == device_col, jnp.bitwise_xor(within, 1), within)
    partner_slot = shuffled[peer_index, device_col * PEER + paired]
    partner_value = peer_index * TILE_DEV + partner_slot
    rows_index = jnp.broadcast_to(device_col, (N_TRACK, TILE_DEV))
    table = jnp.zeros((N_TRACK, TILE_DEV), jnp.int32).at[rows_index, shuffled].set(partner_value)
    return table.reshape(-1)


def touch_ends(array, key, low, high):
    longest = array.shape.index(max(array.shape))
    spots = []
    for shift in (0, 1):
        where = [jax.random.randint(jax.random.fold_in(key, axis), (), 0, length) for axis, length in enumerate(array.shape)]
        where[longest] = (where[longest] + shift) % array.shape[longest]
        spots.append(tuple(where))
    return array.at[spots[0]].set(low).at[spots[1]].set(high)


def shard_levels(rng, shape, pieces, smallest, largest):
    def one(dim, shards_of):
        steps = jax.random.uniform(jax.random.fold_in(jax.random.fold_in(rng, 6), dim), (shards_of,), jnp.float32, smallest / len(pieces), largest / len(pieces))
        return jnp.repeat(jnp.exp(steps), shape[dim] // shards_of).reshape((-1,) + (1,) * (len(shape) - dim - 1))

    factor_of = one(*pieces[0])
    for cut in pieces[1:]:
        factor_of = factor_of * one(*cut)
    return factor_of


def scatter_about(key, extent, spread, bound, pieces=(), kind=jnp.bfloat16):
    loudness = shard_levels(key, extent, pieces, -0.22, 0.18) if pieces else 1.0
    array = jax.random.normal(key, extent, jnp.float32) * spread * loudness
    return jnp.minimum(jnp.maximum(array, -bound), bound).astype(kind)


def setup_inputs(seed: int = 0) -> dict:
    key_list = jax.random.split(jax.random.key(seed), 6)
    jac = scatter_about(key_list[0], (TILES, P_SIZE, W), P_SIZE ** -0.5, 1.75, ((0, 64), (2, 4)), jnp.float32)
    obs = scatter_about(key_list[1], (TILES, W), 1.0, 6.0, ((0, 64), (1, 4)), jnp.float32)
    match = draw_match(jax.random.fold_in(key_list[5], 71), 0)
    tile_knot = touch_ends(jax.random.randint(key_list[3], (TILES,), 0, KNOT_DEV), jax.random.fold_in(key_list[3], 1), 0, KNOT_DEV - 1).astype(jnp.int32)
    tile_frac = jnp.clip(1.0 * jax.random.uniform(key_list[4], (TILES,), jnp.float32) ** shard_levels(key_list[4], (TILES,), ((0, 64),), -0.2, 0.2), 0.0, 1.0)
    return {"jac": jac, "obs": obs, "match": match, "tile_knot": tile_knot, "tile_frac": tile_frac}


damping = 1.0


def reference(jac, obs, match, tile_knot, tile_frac):
    highest = lax.Precision.HIGHEST
    params = jac.shape[1]
    tile_count = jac.shape[0]
    owner_track = jnp.arange(tile_count, dtype=jnp.int32) // TILE_DEV
    knot_index = (owner_track * KNOT_DEV + tile_knot).astype(jnp.int32)
    weight_high = tile_frac
    weight_low = 1.0 - tile_frac

    def forward(knot_field):
        padded = jnp.concatenate([knot_field, jnp.zeros((params, 1), jnp.float32)], axis=1)
        interp = padded[:, knot_index] * weight_low + padded[:, knot_index + 1] * weight_high
        predicted = jnp.einsum("ipw,pi->iw", jac, interp, precision=highest)
        return predicted - predicted[match]

    def adjoint(residual_rows):
        partial_value = jnp.einsum("ipw,iw->pi", jac, residual_rows, precision=highest)
        totals = jnp.zeros((params, KNOTS + 1), jnp.float32)
        totals = totals.at[:, knot_index].add(partial_value * weight_low)
        totals = totals.at[:, knot_index + 1].add(partial_value * weight_high)
        return totals[:, :KNOTS]

    misfit = obs - obs[match]
    knot_field = jnp.zeros((params, KNOTS), jnp.float32)
    tie_residual = misfit
    gradient = adjoint(tie_residual)
    direction = gradient
    slope_norm = jnp.sum(gradient * gradient)
    for iteration in range(ITERS):
        change = forward(direction)
        curvature = 0.5 * jnp.sum(change * change) + damping * jnp.sum(direction * direction)
        step_length = slope_norm / curvature
        knot_field = knot_field + step_length * direction
        tie_residual = tie_residual - step_length * change
        gradient = adjoint(tie_residual) - damping * knot_field
        new_norm = jnp.sum(gradient * gradient)
        direction = gradient + (new_norm / slope_norm) * direction
        slope_norm = new_norm
    return knot_field, tie_residual
```

```python
import functools

import jax
import jax.numpy as jnp
from jax import lax
from jax.experimental import pallas as pl
from jax.experimental.pallas import tpu as pltpu
from jax.sharding import PartitionSpec as P

KNOT_DEV = 128
ITERS = 4
LANES = 128
ROWS = 16
MESH = pl.DeviceIdType.MESH
F32 = jnp.float32
BF16 = jnp.bfloat16

damping = 1.0


def split3(value):
    high = value.astype(BF16)
    rest = value - high.astype(F32)
    mid = rest.astype(BF16)
    low = (rest - mid.astype(F32)).astype(BF16)
    return high, mid, low


def iota(shape, dim):
    return lax.broadcasted_iota(jnp.int32, shape, dim)


def kernel(
    n_track, n_det,
    jac_hbm, obs_ref, match_ref, knot_ref, frac_ref,
    x_out, r_out,
    jac_in, jac_t, sel, sel_t, hot, weight, pred, arrived, fd_ref, r_ref, spread_ref, upd_ref,
    det_send, det_got, prev_got, next_got, gam_send, gam_got, q1_send, q1_got, q2_send, q2_got,
    jac_sem, a_send, a_recv, d_send, d_recv, e_recv, h_recv, g_ssem, g_rsem, q1_ssem, q1_rsem, q2_ssem, q2_rsem,
):
    params, tiles, width = jac_hbm.shape
    me = lax.axis_index("track")
    my_det = lax.axis_index("det")
    per = tiles // n_track
    chunks = tiles // LANES

    load_jac = pltpu.make_async_copy(jac_hbm, jac_in, jac_sem)
    load_jac.start()

    def peer_of(step):
        return lax.rem(me + step, n_track)

    ahead = lax.rem(me + 1, n_track)
    behind = lax.rem(me + n_track - 1, n_track)

    barrier = pltpu.get_barrier_semaphore()

    def greet(step, carry):
        pl.semaphore_signal(barrier, inc=1, device_id=(peer_of(step), my_det), device_id_type=MESH)
        return carry

    lax.fori_loop(1, n_track, greet, 0)
    for off in range(1, n_det):
        other = lax.rem(my_det + off, n_det)
        for track in (me, ahead, behind):
            pl.semaphore_signal(barrier, inc=1, device_id=(track, other), device_id_type=MESH)

    match = match_ref[...]
    shift = tiles.bit_length() - 1
    dest = lax.shift_right_logical(match, jnp.full_like(match, shift))
    slot = jnp.bitwise_and(match, tiles - 1)
    own = iota((1, tiles), 1)
    same = 2 * jnp.minimum(own, slot) + jnp.where(own > slot, 1, 0)
    key = jnp.where(dest > me, own, jnp.where(dest < me, slot, same))
    full = (dest * (2 * tiles) + key).astype(F32)
    full_col = jnp.transpose(jnp.broadcast_to(full, (8, tiles)))[:, 0:1]
    place = jnp.zeros((1, tiles), F32)
    for c in range(chunks):
        less = jnp.where(full_col[c * LANES:(c + 1) * LANES] < full, 1.0, 0.0)
        place = place + jnp.sum(less, axis=0, keepdims=True)
    place_col = jnp.transpose(jnp.broadcast_to(place, (8, tiles)))[:, 0:1]
    for c in range(chunks):
        rows = slice(c * LANES, (c + 1) * LANES)
        row_no = (iota((LANES, tiles), 0) + c * LANES).astype(F32)
        sel_t[rows] = jnp.where(row_no == place, 1.0, 0.0).astype(BF16)
        lane_no = iota((LANES, tiles), 1).astype(F32)
        sel[rows] = jnp.where(lane_no == place_col[rows], 1.0, 0.0).astype(BF16)

    def pick(matrix, value):
        parts = jnp.concatenate(split3(value), axis=1)
        out = jnp.dot(matrix[...], parts, preferred_element_type=F32)
        w = value.shape[1]
        return (out[:, :w] + out[:, w:2 * w]) + out[:, 2 * w:]

    pred[0] = pick(sel_t, obs_ref[...])

    def exchange_start(r):
        mine = pred[r, pl.ds(pl.multiple_of(me * per, per), per), :]
        up = pltpu.roll(mine, per - 1, 0)
        down = pltpu.roll(mine, 1, 0)
        odd = jnp.bitwise_and(iota(mine.shape, 0), 1)
        arrived[r, pl.ds(pl.multiple_of(me * per, per), per), :] = jnp.where(odd == 1, down, up)

        def send(step, carry):
            peer = peer_of(step)
            pltpu.make_async_remote_copy(
                src_ref=pred.at[r, pl.ds(pl.multiple_of(peer * per, per), per), :],
                dst_ref=arrived.at[r, pl.ds(pl.multiple_of(me * per, per), per), :],
                send_sem=a_send.at[r], recv_sem=a_recv.at[r],
                device_id=(peer, my_det), device_id_type=MESH,
            ).start()
            return carry

        lax.fori_loop(1, n_track, send, 0)

    def wait_bytes(buffer, sem):
        pltpu.make_async_copy(buffer, buffer, sem).wait()

    def exchange_wait(r):
        wait_bytes(arrived.at[r, pl.ds(0, tiles - per), :], a_recv.at[r])

    def row_start(k, source, target, ssem, rsem):
        def send(step, carry):
            pltpu.make_async_remote_copy(
                src_ref=source.at[k], dst_ref=target.at[k, me],
                send_sem=ssem.at[k], recv_sem=rsem.at[k],
                device_id=(peer_of(step), my_det), device_id_type=MESH,
            ).start()
            return carry

        target[k, me] = source[k]
        lax.fori_loop(1, n_track, send, 0)

    def row_wait(k, target, rsem):
        wait_bytes(target.at[k, pl.ds(0, n_track - 1)], rsem.at[k])
        total = jnp.sum(target[k], axis=0)
        return jnp.sum(total, axis=1, keepdims=True)

    pl.semaphore_wait(barrier, (n_track - 1) + 3 * (n_det - 1))
    exchange_start(0)

    load_jac.wait()

    def order_jac(p, carry):
        jac_t[p] = jnp.transpose(pick(sel_t, jac_in[p]))
        return carry

    lax.fori_loop(0, params, order_jac, 0)
    frac_parts = [part.astype(F32) for part in split3(frac_ref[...])]
    table = jnp.concatenate([knot_ref[...].astype(F32)] + frac_parts + [jnp.zeros((ROWS - 4, tiles), F32)], axis=0)
    table = jnp.dot(table.astype(BF16), sel[...], preferred_element_type=F32)
    knot = table[0:1]
    frac = (table[1:2] + table[2:3]) + table[3:4]
    weight[0:1] = 1.0 - frac
    weight[1:2] = frac
    hot[...] = jnp.where(iota((LANES, tiles), 0).astype(F32) == knot, 1.0, 0.0).astype(BF16)
    spread_ref[...] = jnp.zeros_like(spread_ref)

    eye = iota((ROWS, LANES), 0) == iota((ROWS, LANES), 1)
    lane = iota((ROWS, LANES), 1)
    sub = iota((ROWS, LANES), 0)

    def to_row(col):
        return jnp.sum(jnp.where(eye, col, 0.0), axis=0, keepdims=True)

    def to_col(row):
        return jnp.sum(jnp.where(eye, row, 0.0), axis=1, keepdims=True)

    def adjoint_start(r):
        for c in range(chunks):
            cols = slice(c * LANES, (c + 1) * LANES)
            turned = jnp.transpose(upd_ref[cols, :])
            for p in range(params):
                spread_ref[p:p + 1, cols] = jnp.sum(jac_t[p, :, cols] * turned, axis=0, keepdims=True)
        sums = spread_ref[...]
        parts = split3(sums * weight[0:1]) + split3(sums * weight[1:2])
        out = lax.dot_general(
            jnp.concatenate(parts, axis=0), hot[...], (((1,), (1,)), ((), ())), preferred_element_type=F32
        )
        low = (out[0:16] + out[16:32]) + out[32:48]
        high = (out[48:64] + out[64:80]) + out[80:96]
        moved = pltpu.roll(high, 1, 1)
        spill = to_row(moved[:, 0:1])
        own_sum = low + jnp.where(lane > 0, moved, 0.0)
        first = to_row(own_sum[:, 0:1])
        own_sum = own_sum + jnp.where(sub == 12, spill, 0.0) + jnp.where(sub == 13, first, 0.0)
        det_send[r] = own_sum
        det_got[r, my_det] = own_sum
        for off in range(1, n_det):
            pltpu.make_async_remote_copy(
                src_ref=det_send.at[r], dst_ref=det_got.at[r, my_det],
                send_sem=d_send.at[r], recv_sem=d_recv.at[r],
                device_id=(me, lax.rem(my_det + off, n_det)), device_id_type=MESH,
            ).start()
        for off in range(n_det):
            other = lax.rem(my_det + off, n_det)
            for track, target, rsem in ((ahead, prev_got, e_recv), (behind, next_got, h_recv)):
                pltpu.make_async_remote_copy(
                    src_ref=det_send.at[r, pl.ds(8, 8), :], dst_ref=target.at[r, my_det],
                    send_sem=d_send.at[r], recv_sem=rsem.at[r],
                    device_id=(track, other), device_id_type=MESH,
                ).start()

    def adjoint_wait(r):
        wait_bytes(det_got.at[r, pl.ds(0, n_det - 1)], d_recv.at[r])
        wait_bytes(prev_got.at[r], e_recv.at[r])
        wait_bytes(next_got.at[r], h_recv.at[r])
        total = jnp.sum(det_got[r], axis=0)
        before = jnp.sum(prev_got[r], axis=0)[4:5]
        after = jnp.sum(next_got[r], axis=0)[5:6]
        carried = jnp.where(me > 0, to_col(before), 0.0)
        beyond = jnp.where(me < n_track - 1, to_col(total[12:13] + after), 0.0)
        main = jnp.where(sub < params, total, 0.0) + jnp.where(lane == 0, carried, 0.0)
        return jnp.concatenate([main, jnp.where(lane == 0, beyond, 0.0)], axis=1)

    def forward(r, field):
        later = pltpu.roll(field, 2 * LANES - 1, 1)
        parts = split3(field[:, :LANES]) + split3(later[:, :LANES])
        out = jnp.dot(jnp.concatenate(parts, axis=0), hot[...], preferred_element_type=F32)
        low = (out[0:16] + out[16:32]) + out[32:48]
        high = (out[48:64] + out[64:80]) + out[80:96]
        interp = low * weight[0:1] + high * weight[1:2]
        for c in range(chunks):
            cols = slice(c * LANES, (c + 1) * LANES)
            total = jac_t[0, :, cols] * interp[0:1, cols]
            for p in range(1, params):
                total = total + jac_t[p, :, cols] * interp[p:p + 1, cols]
            pred[r, cols, :] = jnp.transpose(total)

    exchange_wait(0)
    upd_ref[...] = pred[0] - arrived[0]
    r_ref[...] = upd_ref[...]
    adjoint_start(0)
    gradient = adjoint_wait(0)

    direction = swept = knots = None
    previous = None
    for k in range(ITERS):
        r = k + 1
        forward(r, gradient)
        exchange_start(r)
        squares = gradient[:, :LANES]
        gam_send[k] = jnp.sum(squares * squares, axis=0, keepdims=True)
        row_start(k, gam_send, gam_got, g_ssem, g_rsem)
        exchange_wait(r)
        norm = row_wait(k, gam_got, g_rsem)
        change = pred[r] - arrived[r]
        upd_ref[...] = change
        if k == 0:
            direction = gradient
        else:
            beta = norm / previous
            direction = gradient + beta * direction
            change = change + beta * fd_ref[...]
        fd_ref[...] = change
        held = direction[:, :LANES]
        partial = 0.5 * jnp.sum(change * change, axis=0, keepdims=True)
        partial = partial + (damping / n_det) * jnp.sum(held * held, axis=0, keepdims=True)
        q1_send[k] = partial
        q1_got[k, my_det] = partial
        for off in range(1, n_det):
            pltpu.make_async_remote_copy(
                src_ref=q1_send.at[k], dst_ref=q1_got.at[k, my_det],
                send_sem=q1_ssem.at[k], recv_sem=q1_rsem.at[k],
                device_id=(me, lax.rem(my_det + off, n_det)), device_id_type=MESH,
            ).start()
        if k < ITERS - 1:
            adjoint_start(r)
        wait_bytes(q1_got.at[k, pl.ds(0, n_det - 1)], q1_rsem.at[k])
        q2_send[k] = jnp.sum(q1_got[k], axis=0)
        row_start(k, q2_send, q2_got, q2_ssem, q2_rsem)
        if k < ITERS - 1:
            applied = adjoint_wait(r) + damping * gradient
            swept = applied if k == 0 else applied + beta * swept
        else:
            r_ref[...] = pick(sel, r_ref[...])
            upd_ref[...] = pick(sel, fd_ref[...])
        step = norm / row_wait(k, q2_got, q2_rsem)
        knots = step * direction if k == 0 else knots + step * direction
        if k < ITERS - 1:
            r_ref[...] = r_ref[...] - step * fd_ref[...]
            gradient = gradient - step * swept
            previous = norm
        else:
            r_out[...] = r_ref[...] - step * upd_ref[...]
    x_out[...] = knots[:params, :LANES]

    for r in range(ITERS + 1):
        wait_bytes(pred.at[r, pl.ds(0, tiles - per), :], a_send.at[r])
    for r in range(ITERS):
        wait_bytes(det_got.at[r, pl.ds(0, n_det - 1)], d_send.at[r])
        wait_bytes(prev_got.at[r], d_send.at[r])
        wait_bytes(next_got.at[r], d_send.at[r])
        wait_bytes(gam_got.at[r, pl.ds(0, n_track - 1)], g_ssem.at[r])
        wait_bytes(q1_got.at[r, pl.ds(0, n_det - 1)], q1_ssem.at[r])
        wait_bytes(q2_got.at[r, pl.ds(0, n_track - 1)], q2_ssem.at[r])


def local(n_track, n_det, jac, obs, match, tile_knot, tile_frac):
    tiles, params, width = jac.shape
    rounds = ITERS + 1
    dma = pltpu.SemaphoreType.DMA
    vmem = pl.BlockSpec(memory_space=pltpu.VMEM)
    row = (1, tiles)
    return pl.pallas_call(
        functools.partial(kernel, n_track, n_det),
        out_shape=(
            jax.ShapeDtypeStruct((params, KNOT_DEV), F32),
            jax.ShapeDtypeStruct((tiles, width), F32),
        ),
        in_specs=[pl.BlockSpec(memory_space=pl.ANY), vmem, vmem, vmem, vmem],
        out_specs=(vmem, vmem),
        scratch_shapes=[
            pltpu.VMEM((params, tiles, width), F32),
            pltpu.VMEM((params, width, tiles), F32),
            pltpu.VMEM((tiles, tiles), BF16),
            pltpu.VMEM((tiles, tiles), BF16),
            pltpu.VMEM((KNOT_DEV, tiles), BF16),
            pltpu.VMEM((8, tiles), F32),
            pltpu.VMEM((rounds, tiles, width), F32),
            pltpu.VMEM((rounds, tiles, width), F32),
            pltpu.VMEM((tiles, width), F32),
            pltpu.VMEM((tiles, width), F32),
            pltpu.VMEM((ROWS, tiles), F32),
            pltpu.VMEM((tiles, width), F32),
            pltpu.VMEM((ITERS, ROWS, KNOT_DEV), F32),
            pltpu.VMEM((ITERS, n_det, ROWS, KNOT_DEV), F32),
            pltpu.VMEM((ITERS, n_det, 8, KNOT_DEV), F32),
            pltpu.VMEM((ITERS, n_det, 8, KNOT_DEV), F32),
            pltpu.VMEM((ITERS, 1, LANES), F32),
            pltpu.VMEM((ITERS, n_track, 1, LANES), F32),
            pltpu.VMEM((ITERS, 1, LANES), F32),
            pltpu.VMEM((ITERS, n_det, 1, LANES), F32),
            pltpu.VMEM((ITERS, 1, LANES), F32),
            pltpu.VMEM((ITERS, n_track, 1, LANES), F32),
            dma, dma((rounds,)), dma((rounds,)),
            dma((ITERS,)), dma((ITERS,)), dma((ITERS,)), dma((ITERS,)),
            dma((ITERS,)), dma((ITERS,)), dma((ITERS,)), dma((ITERS,)), dma((ITERS,)), dma((ITERS,)),
        ],
        compiler_params=pltpu.CompilerParams(
            collective_id=0, has_side_effects=True, vmem_limit_bytes=48 * 1024 * 1024
        ),
    )(
        jnp.transpose(jac, (1, 0, 2)), obs,
        match.reshape(row), tile_knot.reshape(row), tile_frac.reshape(row),
    )


def solution(mesh):
    in_specs = (P("track", None, "det"), P("track", "det"), P("track"), P("track"), P("track"))
    out_specs = (P(None, "track"), P("track", "det"))
    body = functools.partial(local, mesh.shape["track"], mesh.shape["det"])
    return jax.shard_map(body, mesh=mesh, in_specs=in_specs, out_specs=out_specs, check_vma=False)
```

```python
import functools

import jax
import jax.numpy as jnp
from jax import lax
from jax.experimental import pallas as pl
from jax.experimental.pallas import tpu as pltpu
from jax.sharding import PartitionSpec as P

KNOT_DEV = 128
ITERS = 4
LANES = 128
ROWS = 16
MESH = pl.DeviceIdType.MESH
TRACK_DIMS = (4, 8, 2)
F32 = jnp.float32
BF16 = jnp.bfloat16

damping = 1.0


def split3(value):
    high = value.astype(BF16)
    rest = value - high.astype(F32)
    mid = rest.astype(BF16)
    low = (rest - mid.astype(F32)).astype(BF16)
    return high, mid, low


def iota(shape, dim):
    return lax.broadcasted_iota(jnp.int32, shape, dim)


def kernel(
    n_track, n_det,
    jac_hbm, obs_hbm, match_hbm, knot_hbm, frac_hbm,
    x_out, r_out,
    obs_ref, match_ref, knot_ref, frac_ref,
    jac_in, jac_t, sel, sel_t, hot, weight, pred, arrived, fd_ref, r_ref, spread_ref, fg_ref,
    det_send, det_got, prev_got, next_got, gam_send, gam_got, q1_send, q1_got, q2_send, q2_got,
    in_sem, jac_sem, a_send, a_recv, d_send, d_recv, e_recv, h_recv, g_ssem, g_rsem, q1_ssem, q1_rsem, q2_ssem, q2_rsem,
):
    params, tiles, width = jac_hbm.shape
    me = lax.axis_index("track")
    my_det = lax.axis_index("det")
    per = tiles // n_track
    chunks = tiles // LANES

    loads = [
        pltpu.make_async_copy(source, target, in_sem.at[i])
        for i, (source, target) in enumerate(
            ((match_hbm, match_ref), (knot_hbm, knot_ref), (frac_hbm, frac_ref), (obs_hbm, obs_ref))
        )
    ]
    for load in loads:
        load.start()
    load_jac = pltpu.make_async_copy(jac_hbm, jac_in, jac_sem)
    load_jac.start()

    def far_first(index, count):
        half = lax.div(index + 1, 2)
        return lax.rem(count // 2 + half * (1 - 2 * lax.rem(index, 2)) + count, count)

    def far_first_py(index, count):
        half = (index + 1) // 2
        return (count // 2 + half * (1 - 2 * (index % 2))) % count

    n_y, n_z, n_core = TRACK_DIMS
    my_y = lax.div(me, n_z * n_core)
    my_z = lax.rem(lax.div(me, n_core), n_z)
    my_core = lax.rem(me, n_core)

    def peer_of(step):
        y = lax.rem(my_y + far_first(lax.div(step, n_z * n_core), n_y), n_y)
        z = lax.rem(my_z + far_first(lax.rem(lax.div(step, n_core), n_z), n_z), n_z)
        core = lax.rem(my_core + n_core - 1 - lax.rem(step, n_core), n_core)
        return (y * n_z + z) * n_core + core

    ahead = lax.rem(me + 1, n_track)
    behind = lax.rem(me + n_track - 1, n_track)

    barrier = pltpu.get_barrier_semaphore()

    def greet(step, carry):
        pl.semaphore_signal(barrier, inc=1, device_id=(peer_of(step), my_det), device_id_type=MESH)
        return carry

    lax.fori_loop(0, n_track - 1, greet, 0)
    for off in range(1, n_det):
        other = lax.rem(my_det + off, n_det)
        for track in (me, ahead, behind):
            pl.semaphore_signal(barrier, inc=1, device_id=(track, other), device_id_type=MESH)

    for load in loads:
        load.wait()
    match = match_ref[...]
    shift = tiles.bit_length() - 1
    dest = lax.shift_right_logical(match, jnp.full_like(match, shift))
    slot = jnp.bitwise_and(match, tiles - 1)
    own = iota((1, tiles), 1)
    same = 2 * jnp.minimum(own, slot) + jnp.where(own > slot, 1, 0)
    key = jnp.where(dest > me, own, jnp.where(dest < me, slot, same))
    full = (dest * (2 * tiles) + key).astype(F32)
    full_col = jnp.transpose(jnp.broadcast_to(full, (8, tiles)))[:, 0:1]
    place = jnp.zeros((1, tiles), F32)
    for c in range(chunks):
        less = jnp.where(full_col[c * LANES:(c + 1) * LANES] < full, 1.0, 0.0)
        place = place + jnp.sum(less, axis=0, keepdims=True)
    place_col = jnp.transpose(jnp.broadcast_to(place, (8, tiles)))[:, 0:1]
    for c in range(chunks):
        rows = slice(c * LANES, (c + 1) * LANES)
        row_no = (iota((LANES, tiles), 0) + c * LANES).astype(F32)
        sel_t[rows] = jnp.where(row_no == place, 1.0, 0.0).astype(BF16)
        lane_no = iota((LANES, tiles), 1).astype(F32)
        sel[rows] = jnp.where(lane_no == place_col[rows], 1.0, 0.0).astype(BF16)

    def pick(matrix, value):
        parts = jnp.concatenate(split3(value), axis=1)
        out = jnp.dot(matrix[...], parts, preferred_element_type=F32)
        w = value.shape[1]
        return (out[:, :w] + out[:, w:2 * w]) + out[:, 2 * w:]

    pred[0] = pick(sel_t, obs_ref[...])

    def exchange_start(r):
        mine = pred[r, pl.ds(pl.multiple_of(me * per, per), per), :]
        up = pltpu.roll(mine, per - 1, 0)
        down = pltpu.roll(mine, 1, 0)
        odd = jnp.bitwise_and(iota(mine.shape, 0), 1)
        arrived[r, pl.ds(pl.multiple_of(me * per, per), per), :] = jnp.where(odd == 1, down, up)

        def send(step, carry):
            peer = peer_of(step)
            group = lax.div(step, n_z * n_core)
            pltpu.make_async_remote_copy(
                src_ref=pred.at[r, pl.ds(pl.multiple_of(peer * per, per), per), :],
                dst_ref=arrived.at[r, pl.ds(pl.multiple_of(me * per, per), per), :],
                send_sem=a_send.at[r], recv_sem=a_recv.at[r, group],
                device_id=(peer, my_det), device_id_type=MESH,
            ).start()
            return carry

        lax.fori_loop(0, n_track - 1, send, 0)

    def wait_bytes(buffer, sem):
        pltpu.make_async_copy(buffer, buffer, sem).wait()

    def exchange_groups(r):
        for group in range(n_y):
            y = lax.rem(my_y + n_y - far_first_py(group, n_y), n_y)
            rows = pl.ds(pl.multiple_of(y * LANES, LANES), LANES)
            count = LANES if group < n_y - 1 else LANES - per
            wait_bytes(arrived.at[r, pl.ds(0, count), :], a_recv.at[r, group])
            yield rows

    def row_start(k, source, target, ssem, rsem):
        def send(step, carry):
            pltpu.make_async_remote_copy(
                src_ref=source.at[k], dst_ref=target.at[k, me],
                send_sem=ssem.at[k], recv_sem=rsem.at[k],
                device_id=(peer_of(step), my_det), device_id_type=MESH,
            ).start()
            return carry

        target[k, me] = source[k]
        lax.fori_loop(0, n_track - 1, send, 0)

    def row_wait(k, target, rsem):
        wait_bytes(target.at[k, pl.ds(0, n_track - 1)], rsem.at[k])
        return jnp.sum(jnp.sum(target[k], axis=0), axis=1, keepdims=True)

    pl.semaphore_wait(barrier, (n_track - 1) + 3 * (n_det - 1))
    exchange_start(0)

    load_jac.wait()

    def order_jac(p, carry):
        jac_t[p] = jnp.transpose(pick(sel_t, jac_in[p]))
        return carry

    lax.fori_loop(0, params, order_jac, 0)
    frac_parts = [part.astype(F32) for part in split3(frac_ref[...])]
    table = jnp.concatenate([knot_ref[...].astype(F32)] + frac_parts + [jnp.zeros((ROWS - 4, tiles), F32)], axis=0)
    table = jnp.dot(table.astype(BF16), sel[...], preferred_element_type=F32)
    knot = table[0:1]
    frac = (table[1:2] + table[2:3]) + table[3:4]
    weight[0:1] = 1.0 - frac
    weight[1:2] = frac
    hot[...] = jnp.where(iota((LANES, tiles), 0).astype(F32) == knot, 1.0, 0.0).astype(BF16)
    spread_ref[...] = jnp.zeros_like(spread_ref)

    eye = iota((ROWS, LANES), 0) == iota((ROWS, LANES), 1)
    lane = iota((ROWS, LANES), 1)
    sub = iota((ROWS, LANES), 0)

    def to_row(col):
        return jnp.sum(jnp.where(eye, col, 0.0), axis=0, keepdims=True)

    def to_col(row):
        return jnp.sum(jnp.where(eye, row, 0.0), axis=1, keepdims=True)

    def adjoint_part(cols, values):
        turned = jnp.transpose(values)
        for p in range(params):
            spread_ref[p:p + 1, cols] = jnp.sum(jac_t[p, :, cols] * turned, axis=0, keepdims=True)

    def adjoint_start(r):
        sums = spread_ref[...]
        parts = split3(sums * weight[0:1]) + split3(sums * weight[1:2])
        out = lax.dot_general(
            jnp.concatenate(parts, axis=0), hot[...], (((1,), (1,)), ((), ())), preferred_element_type=F32
        )
        low = (out[0:16] + out[16:32]) + out[32:48]
        high = (out[48:64] + out[64:80]) + out[80:96]
        moved = pltpu.roll(high, 1, 1)
        spill = to_row(moved[:, 0:1])
        own_sum = low + jnp.where(lane > 0, moved, 0.0)
        first = to_row(own_sum[:, 0:1])
        own_sum = own_sum + jnp.where(sub == 12, spill, 0.0) + jnp.where(sub == 13, first, 0.0)
        det_send[r] = own_sum
        det_got[r, my_det] = own_sum
        for off in range(1, n_det):
            pltpu.make_async_remote_copy(
                src_ref=det_send.at[r], dst_ref=det_got.at[r, my_det],
                send_sem=d_send.at[r], recv_sem=d_recv.at[r],
                device_id=(me, lax.rem(my_det + off, n_det)), device_id_type=MESH,
            ).start()
        for off in range(n_det):
            other = lax.rem(my_det + off, n_det)
            for track, target, rsem in ((ahead, prev_got, e_recv), (behind, next_got, h_recv)):
                pltpu.make_async_remote_copy(
                    src_ref=det_send.at[r, pl.ds(8, 8), :], dst_ref=target.at[r, my_det],
                    send_sem=d_send.at[r], recv_sem=rsem.at[r],
                    device_id=(track, other), device_id_type=MESH,
                ).start()

    def adjoint_wait(r):
        wait_bytes(det_got.at[r, pl.ds(0, n_det - 1)], d_recv.at[r])
        wait_bytes(prev_got.at[r], e_recv.at[r])
        wait_bytes(next_got.at[r], h_recv.at[r])
        total = jnp.sum(det_got[r], axis=0)
        before = jnp.sum(prev_got[r], axis=0)[4:5]
        after = jnp.sum(next_got[r], axis=0)[5:6]
        carried = jnp.where(me > 0, to_col(before), 0.0)
        beyond = jnp.where(me < n_track - 1, to_col(total[12:13] + after), 0.0)
        main = jnp.where(sub < params, total, 0.0) + jnp.where(lane == 0, carried, 0.0)
        return jnp.concatenate([main, jnp.where(lane == 0, beyond, 0.0)], axis=1)

    def forward(r, field):
        later = pltpu.roll(field, 2 * LANES - 1, 1)
        parts = split3(field[:, :LANES]) + split3(later[:, :LANES])
        out = jnp.dot(jnp.concatenate(parts, axis=0), hot[...], preferred_element_type=F32)
        low = (out[0:16] + out[16:32]) + out[32:48]
        high = (out[48:64] + out[64:80]) + out[80:96]
        interp = low * weight[0:1] + high * weight[1:2]
        for c in range(chunks):
            cols = slice(c * LANES, (c + 1) * LANES)
            total = jac_t[0, :, cols] * interp[0:1, cols]
            for p in range(1, params):
                total = total + jac_t[p, :, cols] * interp[p:p + 1, cols]
            pred[r, cols, :] = jnp.transpose(total)

    for rows in exchange_groups(0):
        misfit = pred[0, rows, :] - arrived[0, rows, :]
        r_ref[rows, :] = misfit
        adjoint_part(rows, misfit)
    adjoint_start(0)
    gradient = adjoint_wait(0)
    forward(1, gradient)
    exchange_start(1)

    def norm_start(k, field):
        main = field[:, :LANES]
        gam_send[k] = jnp.sum(main * main, axis=0, keepdims=True)
        row_start(k, gam_send, gam_got, g_ssem, g_rsem)

    norm_start(0, gradient)
    direction = swept = knots = norm = curve = step = None
    for k in range(ITERS):
        r = k + 1
        last = k == ITERS - 1
        own_part = jnp.zeros((1, LANES), F32)
        cross_part = jnp.zeros((1, LANES), F32)
        for rows in exchange_groups(r):
            change = pred[r, rows, :] - arrived[r, rows, :]
            if k > 0:
                change = fg_ref[rows, :] - step * change
                cross_part = cross_part + 0.5 * jnp.sum(change * fd_ref[rows, :], axis=0, keepdims=True)
            fg_ref[rows, :] = change
            own_part = own_part + 0.5 * jnp.sum(change * change, axis=0, keepdims=True)
            if not last:
                adjoint_part(rows, change)
        main = gradient[:, :LANES]
        share = damping / n_det
        own_part = own_part + share * jnp.sum(main * main, axis=0, keepdims=True)
        if k > 0:
            cross_part = cross_part + share * jnp.sum(main * direction[:, :LANES], axis=0, keepdims=True)
        partial = jnp.concatenate([own_part, cross_part], axis=0)
        q1_send[k] = partial
        q1_got[k, my_det] = partial
        for off in range(1, n_det):
            pltpu.make_async_remote_copy(
                src_ref=q1_send.at[k], dst_ref=q1_got.at[k, my_det],
                send_sem=q1_ssem.at[k], recv_sem=q1_rsem.at[k],
                device_id=(me, lax.rem(my_det + off, n_det)), device_id_type=MESH,
            ).start()
        if not last:
            adjoint_start(r)
        new_norm = row_wait(k, gam_got, g_rsem)
        if k == 0:
            direction = gradient
            fd_ref[...] = fg_ref[...]
        else:
            beta = new_norm / norm
            direction = gradient + beta * direction
            fd_ref[...] = fg_ref[...] + beta * fd_ref[...]
        norm = new_norm
        wait_bytes(q1_got.at[k, pl.ds(0, n_det - 1)], q1_rsem.at[k])
        q2_send[k] = jnp.sum(q1_got[k], axis=0)
        row_start(k, q2_send, q2_got, q2_ssem, q2_rsem)
        if not last:
            applied = adjoint_wait(r) + damping * gradient
            swept = applied if k == 0 else applied + beta * swept
            forward(r + 1, swept)
            exchange_start(r + 1)
        else:
            r_ref[...] = pick(sel, r_ref[...])
            fg_ref[...] = pick(sel, fd_ref[...])
        sums = row_wait(k, q2_got, q2_rsem)
        curve = sums[0:1] if k == 0 else sums[0:1] + beta * (2.0 * sums[1:2] + beta * curve)
        step = norm / curve
        knots = step * direction if k == 0 else knots + step * direction
        if not last:
            gradient = gradient - step * swept
            norm_start(k + 1, gradient)
            r_ref[...] = r_ref[...] - step * fd_ref[...]
        else:
            r_out[...] = r_ref[...] - step * fg_ref[...]
    x_out[...] = knots[:params, :LANES]

    for r in range(ITERS + 1):
        wait_bytes(pred.at[r, pl.ds(0, tiles - per), :], a_send.at[r])
    for r in range(ITERS):
        wait_bytes(det_got.at[r, pl.ds(0, n_det - 1)], d_send.at[r])
        wait_bytes(prev_got.at[r], d_send.at[r])
        wait_bytes(next_got.at[r], d_send.at[r])
        wait_bytes(gam_got.at[r, pl.ds(0, n_track - 1)], g_ssem.at[r])
        wait_bytes(q1_got.at[r, pl.ds(0, n_det - 1)], q1_ssem.at[r])
        wait_bytes(q2_got.at[r, pl.ds(0, n_track - 1)], q2_ssem.at[r])


def local(n_track, n_det, jac, obs, match, tile_knot, tile_frac):
    tiles, params, width = jac.shape
    rounds = ITERS + 1
    dma = pltpu.SemaphoreType.DMA
    vmem = pl.BlockSpec(memory_space=pltpu.VMEM)
    row = (1, tiles)
    return pl.pallas_call(
        functools.partial(kernel, n_track, n_det),
        out_shape=(
            jax.ShapeDtypeStruct((params, KNOT_DEV), F32),
            jax.ShapeDtypeStruct((tiles, width), F32),
        ),
        in_specs=[pl.BlockSpec(memory_space=pltpu.HBM)] * 5,
        out_specs=(vmem, vmem),
        scratch_shapes=[
            pltpu.VMEM((tiles, width), F32),
            pltpu.VMEM(row, jnp.int32),
            pltpu.VMEM(row, jnp.int32),
            pltpu.VMEM(row, F32),
            pltpu.VMEM((params, tiles, width), F32),
            pltpu.VMEM((params, width, tiles), F32),
            pltpu.VMEM((tiles, tiles), BF16),
            pltpu.VMEM((tiles, tiles), BF16),
            pltpu.VMEM((KNOT_DEV, tiles), BF16),
            pltpu.VMEM((8, tiles), F32),
            pltpu.VMEM((rounds, tiles, width), F32),
            pltpu.VMEM((rounds, tiles, width), F32),
            pltpu.VMEM((tiles, width), F32),
            pltpu.VMEM((tiles, width), F32),
            pltpu.VMEM((ROWS, tiles), F32),
            pltpu.VMEM((tiles, width), F32),
            pltpu.VMEM((ITERS, ROWS, KNOT_DEV), F32),
            pltpu.VMEM((ITERS, n_det, ROWS, KNOT_DEV), F32),
            pltpu.VMEM((ITERS, n_det, 8, KNOT_DEV), F32),
            pltpu.VMEM((ITERS, n_det, 8, KNOT_DEV), F32),
            pltpu.VMEM((ITERS, 1, LANES), F32),
            pltpu.VMEM((ITERS, n_track, 1, LANES), F32),
            pltpu.VMEM((ITERS, 2, LANES), F32),
            pltpu.VMEM((ITERS, n_det, 2, LANES), F32),
            pltpu.VMEM((ITERS, 2, LANES), F32),
            pltpu.VMEM((ITERS, n_track, 2, LANES), F32),
            dma((4,)), dma, dma((rounds,)), dma((rounds, TRACK_DIMS[0])),
            dma((ITERS,)), dma((ITERS,)), dma((ITERS,)), dma((ITERS,)),
            dma((ITERS,)), dma((ITERS,)), dma((ITERS,)), dma((ITERS,)), dma((ITERS,)), dma((ITERS,)),
        ],
        compiler_params=pltpu.CompilerParams(
            collective_id=0, has_side_effects=True, vmem_limit_bytes=67043328
        ),
    )(
        jnp.transpose(jac, (1, 0, 2)), obs,
        match.reshape(row), tile_knot.reshape(row), tile_frac.reshape(row),
    )


def solution(mesh):
    in_specs = (P("track", None, "det"), P("track", "det"), P("track"), P("track"), P("track"))
    out_specs = (P(None, "track"), P("track", "det"))
    body = functools.partial(local, mesh.shape["track"], mesh.shape["det"])
    return jax.shard_map(body, mesh=mesh, in_specs=in_specs, out_specs=out_specs, check_vma=False)
```

```python
import functools

import jax
import jax.numpy as jnp
from jax import lax
from jax.experimental import pallas as pl
from jax.experimental.pallas import tpu as pltpu
from jax.sharding import PartitionSpec as P

KNOT_DEV = 128
ITERS = 4
LANES = 128
ROWS = 16
MESH = pl.DeviceIdType.MESH
TRACK_DIMS = (4, 8, 2)
F32 = jnp.float32
BF16 = jnp.bfloat16

damping = 1.0


def split3(value):
    high = value.astype(BF16)
    rest = value - high.astype(F32)
    mid = rest.astype(BF16)
    low = (rest - mid.astype(F32)).astype(BF16)
    return high, mid, low


def iota(shape, dim):
    return lax.broadcasted_iota(jnp.int32, shape, dim)


def kernel(
    n_track, n_det,
    jac_hbm, obs_hbm, match_hbm, knot_hbm, frac_hbm,
    x_out, r_out,
    obs_ref, match_ref, knot_ref, frac_ref,
    jac_in, jac_t, sel, sel_t, hot, weight, pred, arrived, fd_ref, r_ref, spread_ref, interp_ref, fg_ref,
    det_send, det_got, edge_send, prev_got, next_got,
    g1_send, g1_got, g2_send, g2_got, q1_send, q1_got, q2_send, q2_got,
    in_sem, jac_sem, a_send, a_recv, d_send, d_recv, e_send, e_recv, h_recv,
    g1_ssem, g1_rsem, g2_ssem, g2_rsem, q1_ssem, q1_rsem, q2_ssem, q2_rsem,
):
    params, tiles, width = jac_hbm.shape
    me = lax.axis_index("track")
    my_det = lax.axis_index("det")
    per = tiles // n_track
    chunks = tiles // LANES

    def far_first(index, count):
        half = lax.div(index + 1, 2)
        return lax.rem(count // 2 + half * (1 - 2 * lax.rem(index, 2)) + count, count)

    def far_first_py(index, count):
        half = (index + 1) // 2
        return (count // 2 + half * (1 - 2 * (index % 2))) % count

    n_y, n_z, n_core = TRACK_DIMS
    my_y = lax.div(me, n_z * n_core)
    my_z = lax.rem(lax.div(me, n_core), n_z)
    my_core = lax.rem(me, n_core)

    def peer_of(step):
        y = lax.rem(my_y + far_first(lax.div(step, n_z * n_core), n_y), n_y)
        z = lax.rem(my_z + far_first(lax.rem(lax.div(step, n_core), n_z), n_z), n_z)
        core = lax.rem(my_core + n_core - 1 - lax.rem(step, n_core), n_core)
        return (y * n_z + z) * n_core + core

    ahead = lax.rem(me + 1, n_track)
    behind = lax.rem(me + n_track - 1, n_track)

    others_y = [lax.rem(my_y + far_first_py(i, n_y), n_y) for i in range(n_y - 1)]
    others_det = [lax.rem(my_det + far_first_py(i, n_det), n_det) for i in range(n_det - 1)]

    def at(y, z, core):
        return (y * n_z + z) * n_core + core

    peers_y = [(at(y, my_z, my_core), my_det) for y in others_y]
    peers_x = [(me, det) for det in others_det]
    peers_xy = [(at(y, my_z, my_core), det) for y in others_y for det in others_det] + peers_y + peers_x
    peers_z = [
        (at(my_y, lax.rem(my_z + far_first_py(i, n_z), n_z), lax.rem(my_core + core, n_core)), my_det)
        for i in range(n_z) for core in reversed(range(n_core)) if i < n_z - 1 or core > 0
    ]
    edges = [(track, det) for track in (ahead, behind) for det in others_det + [my_det]]

    barrier = pltpu.get_barrier_semaphore()

    def greet(step, carry):
        pl.semaphore_signal(barrier, inc=1, device_id=(peer_of(step), my_det), device_id_type=MESH)
        return carry

    lax.fori_loop(0, n_track - 1, greet, 0)
    cross = len(peers_xy) - len(peers_y)
    for device in peers_xy[:cross - len(peers_x)] + peers_x + edges[:n_det - 1] + edges[n_det:2 * n_det - 1]:
        pl.semaphore_signal(barrier, inc=1, device_id=device, device_id_type=MESH)

    loads = [
        pltpu.make_async_copy(source, target, in_sem.at[i])
        for i, (source, target) in enumerate(
            ((match_hbm, match_ref), (knot_hbm, knot_ref), (frac_hbm, frac_ref), (obs_hbm, obs_ref))
        )
    ]
    for load in loads:
        load.start()
    load_jac = pltpu.make_async_copy(jac_hbm, jac_in, jac_sem)
    load_jac.start()

    for load in loads:
        load.wait()
    match = match_ref[...]
    shift = tiles.bit_length() - 1
    dest = lax.shift_right_logical(match, jnp.full_like(match, shift))
    slot = jnp.bitwise_and(match, tiles - 1)
    own = iota((1, tiles), 1)
    same = 2 * jnp.minimum(own, slot) + jnp.where(own > slot, 1, 0)
    key = jnp.where(dest > me, own, jnp.where(dest < me, slot, same))
    full = (dest * (2 * tiles) + key).astype(F32)
    full_col = jnp.transpose(jnp.broadcast_to(full, (8, tiles)))[:, 0:1]
    place = jnp.zeros((1, tiles), F32)
    for c in range(chunks):
        less = jnp.where(full_col[c * LANES:(c + 1) * LANES] < full, 1.0, 0.0)
        place = place + jnp.sum(less, axis=0, keepdims=True)
    place_col = jnp.transpose(jnp.broadcast_to(place, (8, tiles)))[:, 0:1]
    for c in range(chunks):
        rows = slice(c * LANES, (c + 1) * LANES)
        row_no = (iota((LANES, tiles), 0) + c * LANES).astype(F32)
        sel_t[rows] = jnp.where(row_no == place, 1.0, 0.0).astype(BF16)
        lane_no = iota((LANES, tiles), 1).astype(F32)
        sel[rows] = jnp.where(lane_no == place_col[rows], 1.0, 0.0).astype(BF16)

    def pick(matrix, value):
        parts = jnp.concatenate(split3(value), axis=1)
        out = jnp.dot(matrix[...], parts, preferred_element_type=F32)
        w = value.shape[1]
        return (out[:, :w] + out[:, w:2 * w]) + out[:, 2 * w:]

    pred[0] = pick(sel_t, obs_ref[...])

    per_y = n_z * n_core

    def exchange_start(r, group):
        if group == n_y - 1:
            here = pl.ds(pl.multiple_of(me * per, per), per)
            mine = pred[r, here, :]
            up = pltpu.roll(mine, per - 1, 0)
            down = pltpu.roll(mine, 1, 0)
            odd = jnp.bitwise_and(iota(mine.shape, 0), 1)
            arrived[r, here, :] = jnp.where(odd == 1, down, up)

        def send(step, carry):
            peer = peer_of(step)
            pltpu.make_async_remote_copy(
                src_ref=pred.at[r, pl.ds(pl.multiple_of(peer * per, per), per), :],
                dst_ref=arrived.at[r, pl.ds(pl.multiple_of(me * per, per), per), :],
                send_sem=a_send.at[r], recv_sem=a_recv.at[r, group],
                device_id=(peer, my_det), device_id_type=MESH,
            ).start()
            return carry

        lax.fori_loop(group * per_y, min(group * per_y + per_y, n_track - 1), send, 0)

    def wait_bytes(buffer, sem):
        pltpu.make_async_copy(buffer, buffer, sem).wait()

    def exchange_groups(r):
        for group in range(n_y):
            y = lax.rem(my_y + n_y - far_first_py(group, n_y), n_y)
            rows = pl.ds(pl.multiple_of(y * LANES, LANES), LANES)
            count = LANES if group < n_y - 1 else LANES - per
            wait_bytes(arrived.at[r, pl.ds(0, count), :], a_recv.at[r, group])
            yield rows

    def send_rows(k, source, target, slot, ssem, rsem, peers):
        target[k, slot] = source[k]
        for device in peers:
            pltpu.make_async_remote_copy(
                src_ref=source.at[k], dst_ref=target.at[k, slot],
                send_sem=ssem.at[k], recv_sem=rsem.at[k],
                device_id=device, device_id_type=MESH,
            ).start()

    def add_rows(k, target, rsem):
        wait_bytes(target.at[k, pl.ds(0, target.shape[1] - 1)], rsem.at[k])
        return jnp.sum(target[k], axis=0)

    slot_z = my_z * n_core + my_core

    pl.semaphore_wait(barrier, (n_track - 1) + cross + 2 * (n_det - 1))
    for group in range(n_y):
        exchange_start(0, group)

    load_jac.wait()

    def order_jac(p, carry):
        jac_t[p] = jnp.transpose(pick(sel_t, jac_in[p]))
        return carry

    lax.fori_loop(0, params, order_jac, 0)
    frac_parts = [part.astype(F32) for part in split3(frac_ref[...])]
    table = jnp.concatenate([knot_ref[...].astype(F32)] + frac_parts + [jnp.zeros((ROWS - 4, tiles), F32)], axis=0)
    table = jnp.dot(table.astype(BF16), sel[...], preferred_element_type=F32)
    knot = table[0:1]
    frac = (table[1:2] + table[2:3]) + table[3:4]
    weight[0:1] = 1.0 - frac
    weight[1:2] = frac
    weight[2:3] = jnp.where(knot == KNOT_DEV - 1, frac, 0.0)
    weight[3:4] = jnp.where(knot == 0, 1.0 - frac, 0.0)
    hot[...] = jnp.where(iota((LANES, tiles), 0).astype(F32) == knot, 1.0, 0.0).astype(BF16)
    spread_ref[...] = jnp.zeros_like(spread_ref)

    eye = iota((ROWS, LANES), 0) == iota((ROWS, LANES), 1)
    lane = iota((ROWS, LANES), 1)
    sub = iota((ROWS, LANES), 0)

    def to_row(col):
        return jnp.sum(jnp.where(eye, col, 0.0), axis=0, keepdims=True)

    def to_col(row):
        return jnp.sum(jnp.where(eye, row, 0.0), axis=1, keepdims=True)

    def adjoint_part(cols, values):
        turned = jnp.transpose(values)
        for p in range(params):
            spread_ref[p:p + 1, cols] = jnp.sum(jac_t[p, :, cols] * turned, axis=0, keepdims=True)

    def adjoint_start(r):
        sums = spread_ref[...]
        spill = to_row(jnp.sum(sums * weight[2:3], axis=1, keepdims=True))
        first_col = jnp.sum(sums * weight[3:4], axis=1, keepdims=True)
        edge_send[r, 0] = spill
        edge_send[r, 1] = to_row(first_col)
        for side, target, rsem in ((0, prev_got, e_recv), (1, next_got, h_recv)):
            for device in edges[side * n_det:(side + 1) * n_det]:
                pltpu.make_async_remote_copy(
                    src_ref=edge_send.at[r, side], dst_ref=target.at[r, my_det],
                    send_sem=e_send.at[r], recv_sem=rsem.at[r],
                    device_id=device, device_id_type=MESH,
                ).start()
        parts = split3(sums * weight[0:1]) + split3(sums * weight[1:2])
        out = lax.dot_general(
            jnp.concatenate(parts, axis=0), hot[...], (((1,), (1,)), ((), ())), preferred_element_type=F32
        )
        low = (out[0:16] + out[16:32]) + out[32:48]
        high = (out[48:64] + out[64:80]) + out[80:96]
        own_sum = jnp.where(lane > 0, low + pltpu.roll(high, 1, 1), first_col)
        own_sum = own_sum + jnp.where(sub == params, spill, 0.0)
        det_send[r] = own_sum
        det_got[r, my_det] = own_sum
        for device in peers_x:
            pltpu.make_async_remote_copy(
                src_ref=det_send.at[r], dst_ref=det_got.at[r, my_det],
                send_sem=d_send.at[r], recv_sem=d_recv.at[r],
                device_id=device, device_id_type=MESH,
            ).start()

    def adjoint_wait(r):
        wait_bytes(det_got.at[r, pl.ds(0, n_det - 1)], d_recv.at[r])
        wait_bytes(prev_got.at[r], e_recv.at[r])
        wait_bytes(next_got.at[r], h_recv.at[r])
        total = jnp.sum(det_got[r], axis=0)
        before = jnp.sum(prev_got[r], axis=0)
        after = jnp.sum(next_got[r], axis=0)
        carried = jnp.where(me > 0, to_col(before), 0.0)
        beyond = jnp.where(me < n_track - 1, to_col(total[params:params + 1] + after), 0.0)
        main = jnp.where(sub < params, total, 0.0) + jnp.where(lane == 0, carried, 0.0)
        return jnp.concatenate([main, jnp.where(lane == 0, beyond, 0.0)], axis=1)

    def forward(r, field):
        later = pltpu.roll(field, 2 * LANES - 1, 1)
        parts = split3(field[:, :LANES]) + split3(later[:, :LANES])
        out = jnp.dot(jnp.concatenate(parts, axis=0), hot[...], preferred_element_type=F32)
        low = (out[0:16] + out[16:32]) + out[32:48]
        high = (out[48:64] + out[64:80]) + out[80:96]
        interp_ref[...] = low * weight[0:1] + high * weight[1:2]
        for group in range(n_y):
            y = lax.rem(my_y + far_first_py(group, n_y), n_y)
            cols = pl.ds(pl.multiple_of(y * LANES, LANES), LANES)
            total = jac_t[0, :, cols] * interp_ref[0:1, cols]
            for p in range(1, params):
                total = total + jac_t[p, :, cols] * interp_ref[p:p + 1, cols]
            pred[r, cols, :] = jnp.transpose(total)
            exchange_start(r, group)

    for rows in exchange_groups(0):
        misfit = pred[0, rows, :] - arrived[0, rows, :]
        r_ref[rows, :] = misfit
        adjoint_part(rows, misfit)
    adjoint_start(0)
    gradient = adjoint_wait(0)
    forward(1, gradient)

    def norm_start(k, field):
        main = field[:, :LANES]
        g1_send[k] = jnp.sum(main * main, axis=0, keepdims=True)
        send_rows(k, g1_send, g1_got, my_y, g1_ssem, g1_rsem, peers_y)

    def norm_pass(k):
        g2_send[k] = add_rows(k, g1_got, g1_rsem)
        send_rows(k, g2_send, g2_got, slot_z, g2_ssem, g2_rsem, peers_z)

    norm_start(0, gradient)
    direction = swept = knots = norm = curve = step = None
    for k in range(ITERS):
        r = k + 1
        norm_pass(k)
        last = k == ITERS - 1
        own_part = jnp.zeros((1, LANES), F32)
        cross_part = jnp.zeros((1, LANES), F32)
        for rows in exchange_groups(r):
            change = pred[r, rows, :] - arrived[r, rows, :]
            if k > 0:
                change = fg_ref[rows, :] - step * change
                cross_part = cross_part + 0.5 * jnp.sum(change * fd_ref[rows, :], axis=0, keepdims=True)
            fg_ref[rows, :] = change
            own_part = own_part + 0.5 * jnp.sum(change * change, axis=0, keepdims=True)
            if not last:
                adjoint_part(rows, change)
        main = gradient[:, :LANES]
        share = damping / n_det
        own_part = own_part + share * jnp.sum(main * main, axis=0, keepdims=True)
        if k > 0:
            cross_part = cross_part + share * jnp.sum(main * direction[:, :LANES], axis=0, keepdims=True)
        partial = jnp.concatenate([own_part, cross_part], axis=0)
        q1_send[k] = partial
        send_rows(k, q1_send, q1_got, my_y * n_det + my_det, q1_ssem, q1_rsem, peers_xy)
        if not last:
            adjoint_start(r)
        new_norm = jnp.sum(add_rows(k, g2_got, g2_rsem), axis=1, keepdims=True)
        if k == 0:
            direction = gradient
            fd_ref[...] = fg_ref[...]
        else:
            beta = new_norm / norm
            direction = gradient + beta * direction
            fd_ref[...] = fg_ref[...] + beta * fd_ref[...]
        norm = new_norm
        q2_send[k] = add_rows(k, q1_got, q1_rsem)
        send_rows(k, q2_send, q2_got, slot_z, q2_ssem, q2_rsem, peers_z)
        if not last:
            applied = adjoint_wait(r) + damping * gradient
            swept = applied if k == 0 else applied + beta * swept
            forward(r + 1, swept)
        else:
            r_ref[...] = pick(sel, r_ref[...])
            fg_ref[...] = pick(sel, fd_ref[...])
        sums = jnp.sum(add_rows(k, q2_got, q2_rsem), axis=1, keepdims=True)
        curve = sums[0:1] if k == 0 else sums[0:1] + beta * (2.0 * sums[1:2] + beta * curve)
        step = norm / curve
        knots = step * direction if k == 0 else knots + step * direction
        if not last:
            gradient = gradient - step * swept
            norm_start(k + 1, gradient)
            r_ref[...] = r_ref[...] - step * fd_ref[...]
        else:
            r_out[...] = r_ref[...] - step * fg_ref[...]
    x_out[...] = knots[:params, :LANES]

    for r in range(ITERS + 1):
        wait_bytes(pred.at[r, pl.ds(0, tiles - per), :], a_send.at[r])
    for r in range(ITERS):
        wait_bytes(det_got.at[r, pl.ds(0, n_det - 1)], d_send.at[r])
        wait_bytes(prev_got.at[r], e_send.at[r])
        wait_bytes(next_got.at[r], e_send.at[r])
        for target, ssem in ((g1_got, g1_ssem), (g2_got, g2_ssem), (q1_got, q1_ssem), (q2_got, q2_ssem)):
            wait_bytes(target.at[r, pl.ds(0, target.shape[1] - 1)], ssem.at[r])


def local(n_track, n_det, jac, obs, match, tile_knot, tile_frac):
    tiles, params, width = jac.shape
    rounds = ITERS + 1
    n_y = TRACK_DIMS[0]
    dma = pltpu.SemaphoreType.DMA
    vmem = pl.BlockSpec(memory_space=pltpu.VMEM)
    row = (1, tiles)
    operands = (
        jnp.transpose(jac, (1, 0, 2)), obs,
        match.reshape(row), tile_knot.reshape(row), tile_frac.reshape(row),
    )
    return pl.pallas_call(
        functools.partial(kernel, n_track, n_det),
        out_shape=(
            jax.ShapeDtypeStruct((params, KNOT_DEV), F32),
            jax.ShapeDtypeStruct((tiles, width), F32),
        ),
        in_specs=[pl.BlockSpec(memory_space=pltpu.HBM)] * 5,
        out_specs=(vmem, vmem),
        scratch_shapes=[
            pltpu.VMEM((tiles, width), F32),
            pltpu.VMEM(row, jnp.int32),
            pltpu.VMEM(row, jnp.int32),
            pltpu.VMEM(row, F32),
            pltpu.VMEM((params, tiles, width), F32),
            pltpu.VMEM((params, width, tiles), F32),
            pltpu.VMEM((tiles, tiles), BF16),
            pltpu.VMEM((tiles, tiles), BF16),
            pltpu.VMEM((KNOT_DEV, tiles), BF16),
            pltpu.VMEM((8, tiles), F32),
            pltpu.VMEM((rounds, tiles, width), F32),
            pltpu.VMEM((rounds, tiles, width), F32),
            pltpu.VMEM((tiles, width), F32),
            pltpu.VMEM((tiles, width), F32),
            pltpu.VMEM((ROWS, tiles), F32),
            pltpu.VMEM((ROWS, tiles), F32),
            pltpu.VMEM((tiles, width), F32),
            pltpu.VMEM((ITERS, ROWS, KNOT_DEV), F32),
            pltpu.VMEM((ITERS, n_det, ROWS, KNOT_DEV), F32),
            pltpu.VMEM((ITERS, 2, 1, KNOT_DEV), F32),
            pltpu.VMEM((ITERS, n_det, 1, KNOT_DEV), F32),
            pltpu.VMEM((ITERS, n_det, 1, KNOT_DEV), F32),
            pltpu.VMEM((ITERS, 1, LANES), F32),
            pltpu.VMEM((ITERS, n_y, 1, LANES), F32),
            pltpu.VMEM((ITERS, 1, LANES), F32),
            pltpu.VMEM((ITERS, n_track // n_y, 1, LANES), F32),
            pltpu.VMEM((ITERS, 2, LANES), F32),
            pltpu.VMEM((ITERS, n_y * n_det, 2, LANES), F32),
            pltpu.VMEM((ITERS, 2, LANES), F32),
            pltpu.VMEM((ITERS, n_track // n_y, 2, LANES), F32),
            dma((4,)), dma, dma((rounds,)), dma((rounds, n_y)),
        ] + [dma((ITERS,))] * 13,
        compiler_params=pltpu.CompilerParams(
            collective_id=0, has_side_effects=True, vmem_limit_bytes=48 * 1024 * 1024
        ),
    )(*(pltpu.with_memory_space_constraint(value, pltpu.HBM) for value in operands))


def solution(mesh):
    in_specs = (P("track", None, "det"), P("track", "det"), P("track"), P("track"), P("track"))
    out_specs = (P(None, "track"), P("track", "det"))
    body = functools.partial(local, mesh.shape["track"], mesh.shape["det"])
    return jax.shard_map(body, mesh=mesh, in_specs=in_specs, out_specs=out_specs, check_vma=False)
```

```python
import functools

import jax
import jax.numpy as jnp
from jax import lax
from jax.experimental import pallas as pl
from jax.experimental.pallas import tpu as pltpu
from jax.sharding import PartitionSpec as P

KNOT_DEV = 128
ITERS = 4
LANES = 128
ROWS = 16
MESH = pl.DeviceIdType.MESH
TRACK_DIMS = (4, 8, 2)
F32 = jnp.float32
BF16 = jnp.bfloat16

damping = 1.0


def split3(value):
    high = value.astype(BF16)
    rest = value - high.astype(F32)
    mid = rest.astype(BF16)
    low = (rest - mid.astype(F32)).astype(BF16)
    return high, mid, low


def iota(shape, dim):
    return lax.broadcasted_iota(jnp.int32, shape, dim)


def kernel(
    n_track, n_det,
    jac_hbm, obs_hbm, match_hbm, knot_hbm, frac_hbm,
    x_out, r_out,
    obs_ref, match_ref, knot_ref, frac_ref,
    jac_in, jac_t, sel, sel_t, hot, weight, pred, arrived, fd_ref, r_ref, spread_ref, interp_ref, fg_ref,
    det_send, det_got, edge_send, prev_got, next_got,
    g1_send, g1_got, g2_send, g2_got, q1_send, q1_got, q2_send, q2_got,
    in_sem, jac_sem, a_send, a_recv, d_send, d_recv, e_send, e_recv, h_recv,
    g1_ssem, g1_rsem, g2_ssem, g2_rsem, q1_ssem, q1_rsem, q2_ssem, q2_rsem,
):
    params, tiles, width = jac_hbm.shape
    me = lax.axis_index("track")
    my_det = lax.axis_index("det")
    per = tiles // n_track
    chunks = tiles // LANES

    def far_first(index, count):
        half = lax.div(index + 1, 2)
        return lax.rem(count // 2 + half * (1 - 2 * lax.rem(index, 2)) + count, count)

    def far_first_py(index, count):
        half = (index + 1) // 2
        return (count // 2 + half * (1 - 2 * (index % 2))) % count

    n_y, n_z, n_core = TRACK_DIMS
    my_y = lax.div(me, n_z * n_core)
    my_z = lax.rem(lax.div(me, n_core), n_z)
    my_core = lax.rem(me, n_core)

    def peer_of(step):
        y = lax.rem(my_y + far_first(lax.div(step, n_z * n_core), n_y), n_y)
        z = lax.rem(my_z + far_first(lax.rem(lax.div(step, n_core), n_z), n_z), n_z)
        core = lax.rem(my_core + n_core - 1 - lax.rem(step, n_core), n_core)
        return (y * n_z + z) * n_core + core

    ahead = lax.rem(me + 1, n_track)
    behind = lax.rem(me + n_track - 1, n_track)

    others_y = [lax.rem(my_y + far_first_py(i, n_y), n_y) for i in range(n_y - 1)]
    others_det = [lax.rem(my_det + far_first_py(i, n_det), n_det) for i in range(n_det - 1)]

    def at(y, z, core):
        return (y * n_z + z) * n_core + core

    peers_y = [(at(y, my_z, my_core), my_det) for y in others_y]
    peers_x = [(me, det) for det in others_det]
    peers_xy = [(at(y, my_z, my_core), det) for y in others_y for det in others_det] + peers_y + peers_x
    peers_z = [
        (at(my_y, lax.rem(my_z + far_first_py(i, n_z), n_z), lax.rem(my_core + core, n_core)), my_det)
        for i in range(n_z) for core in reversed(range(n_core)) if i < n_z - 1 or core > 0
    ]
    edges = [(track, det) for track in (ahead, behind) for det in others_det + [my_det]]

    barrier = pltpu.get_barrier_semaphore()

    def greet(step, carry):
        pl.semaphore_signal(barrier, inc=1, device_id=(peer_of(step), my_det), device_id_type=MESH)
        return carry

    lax.fori_loop(0, n_track - 1, greet, 0)
    cross = len(peers_xy) - len(peers_y)
    for device in peers_xy[:cross - len(peers_x)] + peers_x + edges[:n_det - 1] + edges[n_det:2 * n_det - 1]:
        pl.semaphore_signal(barrier, inc=1, device_id=device, device_id_type=MESH)

    loads = [
        pltpu.make_async_copy(source, target, in_sem.at[i])
        for i, (source, target) in enumerate(
            ((match_hbm, match_ref), (knot_hbm, knot_ref), (frac_hbm, frac_ref), (obs_hbm, obs_ref))
        )
    ]
    for load in loads:
        load.start()
    load_jac = pltpu.make_async_copy(jac_hbm, jac_in, jac_sem)
    load_jac.start()

    for load in loads:
        load.wait()
    match = match_ref[...]
    shift = tiles.bit_length() - 1
    dest = lax.shift_right_logical(match, jnp.full_like(match, shift))
    slot = jnp.bitwise_and(match, tiles - 1)
    own = iota((1, tiles), 1)
    same = 2 * jnp.minimum(own, slot) + jnp.where(own > slot, 1, 0)
    key = jnp.where(dest > me, own, jnp.where(dest < me, slot, same))
    full = (dest * (2 * tiles) + key).astype(F32)
    full_col = jnp.transpose(jnp.broadcast_to(full, (8, tiles)))[:, 0:1]
    place = jnp.zeros((1, tiles), F32)
    for c in range(chunks):
        less = jnp.where(full_col[c * LANES:(c + 1) * LANES] < full, 1.0, 0.0)
        place = place + jnp.sum(less, axis=0, keepdims=True)
    place_col = jnp.transpose(jnp.broadcast_to(place, (8, tiles)))[:, 0:1]
    for c in range(chunks):
        rows = slice(c * LANES, (c + 1) * LANES)
        row_no = (iota((LANES, tiles), 0) + c * LANES).astype(F32)
        sel_t[rows] = jnp.where(row_no == place, 1.0, 0.0).astype(BF16)
        lane_no = iota((LANES, tiles), 1).astype(F32)
        sel[rows] = jnp.where(lane_no == place_col[rows], 1.0, 0.0).astype(BF16)

    def pick(matrix, value):
        parts = jnp.concatenate(split3(value), axis=1)
        out = jnp.dot(matrix[...], parts, preferred_element_type=F32)
        w = value.shape[1]
        return (out[:, :w] + out[:, w:2 * w]) + out[:, 2 * w:]

    pred[0] = pick(sel_t, obs_ref[...])

    per_y = n_z * n_core

    def exchange_start(r, group):
        if group == n_y - 1:
            here = pl.ds(pl.multiple_of(me * per, per), per)
            mine = pred[r, here, :]
            up = pltpu.roll(mine, per - 1, 0)
            down = pltpu.roll(mine, 1, 0)
            odd = jnp.bitwise_and(iota(mine.shape, 0), 1)
            arrived[r, here, :] = jnp.where(odd == 1, down, up)

        def send(step, carry):
            peer = peer_of(step)
            pltpu.make_async_remote_copy(
                src_ref=pred.at[r, pl.ds(pl.multiple_of(peer * per, per), per), :],
                dst_ref=arrived.at[r, pl.ds(pl.multiple_of(me * per, per), per), :],
                send_sem=a_send.at[r], recv_sem=a_recv.at[r, group],
                device_id=(peer, my_det), device_id_type=MESH,
            ).start()
            return carry

        lax.fori_loop(group * per_y, min(group * per_y + per_y, n_track - 1), send, 0)

    def wait_bytes(buffer, sem):
        pltpu.make_async_copy(buffer, buffer, sem).wait()

    def exchange_groups(r):
        for group in range(n_y):
            y = lax.rem(my_y + n_y - far_first_py(group, n_y), n_y)
            rows = pl.ds(pl.multiple_of(y * LANES, LANES), LANES)
            count = LANES if group < n_y - 1 else LANES - per
            wait_bytes(arrived.at[r, pl.ds(0, count), :], a_recv.at[r, group])
            yield rows

    def send_rows(k, source, target, slot, ssem, rsem, peers):
        target[k, slot] = source[k]
        for device in peers:
            pltpu.make_async_remote_copy(
                src_ref=source.at[k], dst_ref=target.at[k, slot],
                send_sem=ssem.at[k], recv_sem=rsem.at[k],
                device_id=device, device_id_type=MESH,
            ).start()

    def add_rows(k, target, rsem):
        wait_bytes(target.at[k, pl.ds(0, target.shape[1] - 1)], rsem.at[k])
        return jnp.sum(target[k], axis=0)

    slot_z = my_z * n_core + my_core

    pl.semaphore_wait(barrier, (n_track - 1) + cross + 2 * (n_det - 1))
    for group in range(n_y):
        exchange_start(0, group)

    load_jac.wait()

    def order_jac(p, carry):
        jac_t[p] = jnp.transpose(pick(sel_t, jac_in[p]))
        return carry

    lax.fori_loop(0, params, order_jac, 0)
    frac_parts = [part.astype(F32) for part in split3(frac_ref[...])]
    table = jnp.concatenate([knot_ref[...].astype(F32)] + frac_parts + [jnp.zeros((ROWS - 4, tiles), F32)], axis=0)
    table = jnp.dot(table.astype(BF16), sel[...], preferred_element_type=F32)
    knot = table[0:1]
    frac = (table[1:2] + table[2:3]) + table[3:4]
    weight[0:1] = 1.0 - frac
    weight[1:2] = frac
    weight[2:3] = jnp.where(knot == KNOT_DEV - 1, frac, 0.0)
    weight[3:4] = jnp.where(knot == 0, 1.0 - frac, 0.0)
    hot[...] = jnp.where(iota((LANES, tiles), 0).astype(F32) == knot, 1.0, 0.0).astype(BF16)
    spread_ref[...] = jnp.zeros_like(spread_ref)

    eye = iota((ROWS, LANES), 0) == iota((ROWS, LANES), 1)
    lane = iota((ROWS, LANES), 1)
    sub = iota((ROWS, LANES), 0)

    def to_row(col):
        return jnp.sum(jnp.where(eye, col, 0.0), axis=0, keepdims=True)

    def to_col(row):
        return jnp.sum(jnp.where(eye, row, 0.0), axis=1, keepdims=True)

    def adjoint_part(cols, values):
        turned = jnp.transpose(values)
        for p in range(params):
            spread_ref[p:p + 1, cols] = jnp.sum(jac_t[p, :, cols] * turned, axis=0, keepdims=True)

    def ends_start(r):
        sums = spread_ref[...]
        spill = to_row(jnp.sum(sums * weight[2:3], axis=1, keepdims=True))
        first_col = jnp.sum(sums * weight[3:4], axis=1, keepdims=True)
        edge_send[r, 0] = spill
        edge_send[r, 1] = to_row(first_col)
        for side, target, rsem in ((0, prev_got, e_recv), (1, next_got, h_recv)):
            for device in edges[side * n_det:(side + 1) * n_det]:
                pltpu.make_async_remote_copy(
                    src_ref=edge_send.at[r, side], dst_ref=target.at[r, my_det],
                    send_sem=e_send.at[r], recv_sem=rsem.at[r],
                    device_id=device, device_id_type=MESH,
                ).start()
        return spill, first_col

    def sums_start(r, spill, first_col):
        sums = spread_ref[...]
        parts = split3(sums * weight[0:1]) + split3(sums * weight[1:2])
        out = lax.dot_general(
            jnp.concatenate(parts, axis=0), hot[...], (((1,), (1,)), ((), ())), preferred_element_type=F32
        )
        low = (out[0:16] + out[16:32]) + out[32:48]
        high = (out[48:64] + out[64:80]) + out[80:96]
        own_sum = jnp.where(lane > 0, low + pltpu.roll(high, 1, 1), first_col)
        own_sum = own_sum + jnp.where(sub == params, spill, 0.0)
        det_send[r] = own_sum
        det_got[r, my_det] = own_sum
        for device in peers_x:
            pltpu.make_async_remote_copy(
                src_ref=det_send.at[r], dst_ref=det_got.at[r, my_det],
                send_sem=d_send.at[r], recv_sem=d_recv.at[r],
                device_id=device, device_id_type=MESH,
            ).start()

    def sums_wait(r):
        wait_bytes(det_got.at[r, pl.ds(0, n_det - 1)], d_recv.at[r])
        total = jnp.sum(det_got[r], axis=0)
        beyond = jnp.where(me < n_track - 1, to_col(total[params:params + 1]), 0.0)
        main = jnp.where(sub < params, total, 0.0)
        return jnp.concatenate([main, jnp.where(lane == 0, beyond, 0.0)], axis=1)

    def ends_wait(r):
        wait_bytes(prev_got.at[r], e_recv.at[r])
        wait_bytes(next_got.at[r], h_recv.at[r])
        before = jnp.sum(prev_got[r], axis=0)
        after = jnp.sum(next_got[r], axis=0)
        return jnp.where(me > 0, to_col(before), 0.0), jnp.where(me < n_track - 1, to_col(after), 0.0)

    def forward(r, field, meanwhile=None):
        later = pltpu.roll(field, 2 * LANES - 1, 1)
        parts = split3(field[:, :LANES]) + split3(later[:, :LANES])
        out = jnp.dot(jnp.concatenate(parts, axis=0), hot[...], preferred_element_type=F32)
        low = (out[0:16] + out[16:32]) + out[32:48]
        high = (out[48:64] + out[64:80]) + out[80:96]
        interp = low * weight[0:1] + high * weight[1:2]
        if meanwhile is not None:
            meanwhile()
        carried, beyond = ends_wait(r - 1)
        interp_ref[...] = interp + carried * weight[3:4] + beyond * weight[2:3]
        for group in range(n_y):
            y = lax.rem(my_y + far_first_py(group, n_y), n_y)
            cols = pl.ds(pl.multiple_of(y * LANES, LANES), LANES)
            total = jac_t[0, :, cols] * interp_ref[0:1, cols]
            for p in range(1, params):
                total = total + jac_t[p, :, cols] * interp_ref[p:p + 1, cols]
            pred[r, cols, :] = jnp.transpose(total)
            exchange_start(r, group)
        ends = [jnp.where(lane == 0, end, 0.0) for end in (carried, beyond)]
        return field + jnp.concatenate(ends, axis=1)

    for rows in exchange_groups(0):
        misfit = pred[0, rows, :] - arrived[0, rows, :]
        r_ref[rows, :] = misfit
        adjoint_part(rows, misfit)
    sums_start(0, *ends_start(0))
    gradient = forward(1, sums_wait(0))

    def norm_start(k, field):
        main = field[:, :LANES]
        g1_send[k] = jnp.sum(main * main, axis=0, keepdims=True)
        send_rows(k, g1_send, g1_got, my_y, g1_ssem, g1_rsem, peers_y)

    def norm_pass(k):
        g2_send[k] = add_rows(k, g1_got, g1_rsem)
        send_rows(k, g2_send, g2_got, slot_z, g2_ssem, g2_rsem, peers_z)

    norm_start(0, gradient)
    direction = swept = knots = norm = curve = step = None
    for k in range(ITERS):
        r = k + 1
        norm_pass(k)
        last = k == ITERS - 1
        own_part = jnp.zeros((1, LANES), F32)
        cross_part = jnp.zeros((1, LANES), F32)
        for rows in exchange_groups(r):
            change = pred[r, rows, :] - arrived[r, rows, :]
            if k > 0:
                change = fg_ref[rows, :] - step * change
                cross_part = cross_part + 0.5 * jnp.sum(change * fd_ref[rows, :], axis=0, keepdims=True)
            fg_ref[rows, :] = change
            own_part = own_part + 0.5 * jnp.sum(change * change, axis=0, keepdims=True)
            if not last:
                adjoint_part(rows, change)
        if not last:
            ends = ends_start(r)
        main = gradient[:, :LANES]
        share = damping / n_det
        own_part = own_part + share * jnp.sum(main * main, axis=0, keepdims=True)
        if k > 0:
            cross_part = cross_part + share * jnp.sum(main * direction[:, :LANES], axis=0, keepdims=True)
        partial = jnp.concatenate([own_part, cross_part], axis=0)
        q1_send[k] = partial
        send_rows(k, q1_send, q1_got, my_y * n_det + my_det, q1_ssem, q1_rsem, peers_xy)
        if not last:
            sums_start(r, *ends)
        new_norm = jnp.sum(add_rows(k, g2_got, g2_rsem), axis=1, keepdims=True)
        if k == 0:
            direction = gradient
            fd_ref[...] = fg_ref[...]
        else:
            beta = new_norm / norm
            direction = gradient + beta * direction
            fd_ref[...] = fg_ref[...] + beta * fd_ref[...]
        norm = new_norm

        def pass_on():
            q2_send[k] = add_rows(k, q1_got, q1_rsem)
            send_rows(k, q2_send, q2_got, slot_z, q2_ssem, q2_rsem, peers_z)

        if not last:
            applied = sums_wait(r) + damping * gradient
            swept = forward(r + 1, applied if k == 0 else applied + beta * swept, pass_on)
        else:
            pass_on()
            r_ref[...] = pick(sel, r_ref[...])
            fg_ref[...] = pick(sel, fd_ref[...])
        sums = jnp.sum(add_rows(k, q2_got, q2_rsem), axis=1, keepdims=True)
        curve = sums[0:1] if k == 0 else sums[0:1] + beta * (2.0 * sums[1:2] + beta * curve)
        step = norm / curve
        knots = step * direction if k == 0 else knots + step * direction
        if not last:
            gradient = gradient - step * swept
            norm_start(k + 1, gradient)
            r_ref[...] = r_ref[...] - step * fd_ref[...]
        else:
            r_out[...] = r_ref[...] - step * fg_ref[...]
    x_out[...] = knots[:params, :LANES]

    for r in range(ITERS + 1):
        wait_bytes(pred.at[r, pl.ds(0, tiles - per), :], a_send.at[r])
    for r in range(ITERS):
        wait_bytes(det_got.at[r, pl.ds(0, n_det - 1)], d_send.at[r])
        wait_bytes(prev_got.at[r], e_send.at[r])
        wait_bytes(next_got.at[r], e_send.at[r])
        for target, ssem in ((g1_got, g1_ssem), (g2_got, g2_ssem), (q1_got, q1_ssem), (q2_got, q2_ssem)):
            wait_bytes(target.at[r, pl.ds(0, target.shape[1] - 1)], ssem.at[r])


def put_out(knots, residual, x_out, r_out, sem):
    copies = [
        pltpu.make_async_copy(source, target, sem.at[i])
        for i, (source, target) in enumerate(((residual, r_out), (knots, x_out)))
    ]
    for copy in copies:
        copy.start()
    for copy in copies:
        copy.wait()


def local(n_track, n_det, jac, obs, match, tile_knot, tile_frac):
    tiles, params, width = jac.shape
    rounds = ITERS + 1
    n_y = TRACK_DIMS[0]
    dma = pltpu.SemaphoreType.DMA
    vmem = pl.BlockSpec(memory_space=pltpu.VMEM)
    row = (1, tiles)
    operands = (
        jnp.transpose(jac, (1, 0, 2)), obs,
        match.reshape(row), tile_knot.reshape(row), tile_frac.reshape(row),
    )
    knots, residual = pl.pallas_call(
        functools.partial(kernel, n_track, n_det),
        out_shape=(
            jax.ShapeDtypeStruct((params, KNOT_DEV), F32),
            jax.ShapeDtypeStruct((tiles, width), F32),
        ),
        in_specs=[pl.BlockSpec(memory_space=pltpu.HBM)] * 5,
        out_specs=(vmem, vmem),
        scratch_shapes=[
            pltpu.VMEM((tiles, width), F32),
            pltpu.VMEM(row, jnp.int32),
            pltpu.VMEM(row, jnp.int32),
            pltpu.VMEM(row, F32),
            pltpu.VMEM((params, tiles, width), F32),
            pltpu.VMEM((params, width, tiles), F32),
            pltpu.VMEM((tiles, tiles), BF16),
            pltpu.VMEM((tiles, tiles), BF16),
            pltpu.VMEM((KNOT_DEV, tiles), BF16),
            pltpu.VMEM((8, tiles), F32),
            pltpu.VMEM((rounds, tiles, width), F32),
            pltpu.VMEM((rounds, tiles, width), F32),
            pltpu.VMEM((tiles, width), F32),
            pltpu.VMEM((tiles, width), F32),
            pltpu.VMEM((ROWS, tiles), F32),
            pltpu.VMEM((ROWS, tiles), F32),
            pltpu.VMEM((tiles, width), F32),
            pltpu.VMEM((ITERS, ROWS, KNOT_DEV), F32),
            pltpu.VMEM((ITERS, n_det, ROWS, KNOT_DEV), F32),
            pltpu.VMEM((ITERS, 2, 1, KNOT_DEV), F32),
            pltpu.VMEM((ITERS, n_det, 1, KNOT_DEV), F32),
            pltpu.VMEM((ITERS, n_det, 1, KNOT_DEV), F32),
            pltpu.VMEM((ITERS, 1, LANES), F32),
            pltpu.VMEM((ITERS, n_y, 1, LANES), F32),
            pltpu.VMEM((ITERS, 1, LANES), F32),
            pltpu.VMEM((ITERS, n_track // n_y, 1, LANES), F32),
            pltpu.VMEM((ITERS, 2, LANES), F32),
            pltpu.VMEM((ITERS, n_y * n_det, 2, LANES), F32),
            pltpu.VMEM((ITERS, 2, LANES), F32),
            pltpu.VMEM((ITERS, n_track // n_y, 2, LANES), F32),
            dma((4,)), dma, dma((rounds,)), dma((rounds, n_y)),
        ] + [dma((ITERS,))] * 13,
        compiler_params=pltpu.CompilerParams(
            collective_id=0, has_side_effects=True, vmem_limit_bytes=48 * 1024 * 1024
        ),
    )(*(pltpu.with_memory_space_constraint(value, pltpu.HBM) for value in operands))
    hbm = pl.BlockSpec(memory_space=pltpu.HBM)
    return pl.pallas_call(
        put_out,
        out_shape=(
            jax.ShapeDtypeStruct((params, KNOT_DEV), F32),
            jax.ShapeDtypeStruct((tiles, width), F32),
        ),
        in_specs=[vmem, vmem],
        out_specs=(hbm, hbm),
        scratch_shapes=[dma((2,))],
        compiler_params=pltpu.CompilerParams(vmem_limit_bytes=2 * 1024 * 1024),
    )(knots, residual)


def solution(mesh):
    in_specs = (P("track", None, "det"), P("track", "det"), P("track"), P("track"), P("track"))
    out_specs = (P(None, "track"), P("track", "det"))
    body = functools.partial(local, mesh.shape["track"], mesh.shape["det"])
    return jax.shard_map(body, mesh=mesh, in_specs=in_specs, out_specs=out_specs, check_vma=False)
```
